1024 devices in a mesh: expert: 64 (over x_lo, z, core), blk: 16 (over y, x_hi).
Axes of the slice: x: 4 (x_hi: 2, x_lo: 2; x = x_hi * 2 + x_lo), y: 8, z: 16, core: 2. Of those that a mesh axis runs over, the one named last changes fastest.
Arguments:
- tokens: bfloat16 [32768, 3584], P('expert', 'blk'), may hold values from -6 to 6
- route: int32 [32768, 1], P('expert'), may hold values from 0 to 63; in each aligned block of 512 rows (0 to 511, 512 to 1023, ...) at most 12 rows name the same one
- gate_score: float32 [32768, 1], P('expert'), may hold values from 0.1 to 1
- w_gate: bfloat16 [64, 3584, 2048], P('expert', None, 'blk'), may hold values from -0.09375 to 0.09375
- w_up: bfloat16 [64, 3584, 2048], P('expert', None, 'blk'), may hold values from -0.09375 to 0.09375
- w_down: bfloat16 [64, 2048, 3584], P('expert', 'blk'), may hold values from -0.125 to 0.125
Outputs:
- mixed: bfloat16 [32768, 3584], P('expert', 'blk')
The draws below stay inside these ranges and needn't reach their ends.
Inputs may be any that keep to these rules, and one draw needn't show every extreme that they name: `route`: among the 512 tokens of one index of expert (aligned blocks of rows), no expert is named more than 12 times, a bound that some block reaches.
All inputs are finite; a program needn't handle non-finite values.
Results may differ from the reference program's by a relative error of at most 0.015.
Values may be sent and summed in bfloat16 or wider, within the bound.
A program may use at most 64 MiB of HBM per device.

```python
import math
import jax
import jax.numpy as jnp
import numpy as np
from jax import lax

D = 3584
FF = 2048
TOK_DEV = 512
EXPERTS = 64
CAP = 12
TOKENS = 32768
N_BLK = 16


def steps_of(own_key, shape, split, smallest, high):
    level, own = 1.0, jax.random.fold_in(own_key, 6)
    for dim, shards_of in split:
        steps = jnp.exp(jax.random.uniform(jax.random.fold_in(own, dim), (shards_of,), jnp.float32, smallest / len(split), high / len(split)))
        level = level * jnp.repeat(steps, shape[dim] // shards_of).reshape([-1 if axis == dim else 1 for axis in range(len(shape))])
    return level


def assign_block(own_key, own, number, rows, count, top, bound, skew):
    order = jax.random.permutation(own_key, count)
    heavy_load, usual = portions_of(count, rows * top, bound, skew, True), portions_of(count, rows * top, bound, skew, False)
    places = jnp.arange(count)

    def named(tallies, offset_by):
        used = int((tallies > 0).sum())
        fixed = max(1, used // 4)
        passed = fixed + (places - fixed + offset_by * (used - fixed)) % max(1, count - fixed)
        return jnp.zeros((count,), jnp.int32).at[order[jnp.where(places < fixed, places, passed)]].set(jnp.asarray(tallies, jnp.int32))

    tallies = jnp.where(number % 4 == 0, named(heavy_load, number // 4), named(usual, number - number // 4 - 1))
    mixed = jax.random.permutation(jax.random.fold_in(own, 3), count)
    giver, receiver = mixed[0:count // 2 * 2:2], mixed[1:count // 2 * 2:2]
    room = jnp.minimum(tallies[giver] - 1, bound - tallies[receiver]) // 2
    room = jnp.where((giver == order[0]) | (receiver == order[0]) | (tallies[receiver] == 0), 0, jnp.maximum(room, 0))
    passed = jax.random.randint(jax.random.fold_in(own, 4), (count // 2,), 0, 1 << 20) % (room + 1)
    tallies = tallies.at[giver].add(-passed).at[receiver].add(passed)
    items = jnp.searchsorted(jnp.cumsum(tallies), jnp.arange(rows * top), side="right").astype(jnp.int32)
    table = items.reshape(top, rows).T
    table = table[jax.random.permutation(jax.random.fold_in(own, 1), rows)]
    offset_by = jax.random.randint(jax.random.fold_in(own, 2), (rows, 1), 0, top)
    return jnp.take_along_axis(table, (jnp.arange(top)[None, :] + offset_by) % top, axis=1)


def portions_of(number_of, total, limit, skew, full):
    portions = [(1 << 20) // math.isqrt(grade ** skew) + 1 for grade in range(1, number_of + 1)]
    largest = limit if full else min(limit, max(-(-total // number_of), total * portions[0] // sum(portions)))
    least = 1 if total - largest >= number_of - 1 else 0
    given, rest = [largest] + [least] * (number_of - 1), total - largest - least * (number_of - 1)
    while rest > 0:
        movable = [i for i in range(1, number_of) if given[i] < largest] or [i for i in range(1, number_of) if given[i] < limit]
        whole, remaining = sum([portions[i] for i in movable]), rest
        for i in movable:
            more = min(limit - given[i], max(1, remaining * portions[i] // whole), rest)
            given[i] = given[i] + more
            rest = rest - more
    return np.array(given)


def noise(key, dims, scale, bound, cuts=(), kind=jnp.bfloat16):
    drawn = scale * jax.random.normal(key, dims, jnp.float32)
    if cuts:
        drawn = drawn * steps_of(key, dims, cuts, -0.22, 0.18)
    return jnp.clip(drawn, -bound, bound).astype(kind)


def setup_inputs(seed: int = 0) -> dict:
    key_list = jax.random.split(jax.random.key(seed), 7)
    tokens = noise(key_list[0], (TOKENS, D), 1.0, 6.0, ((0, 64), (1, 16)))
    route_keys = jax.random.split(jax.random.fold_in(key_list[1], 1), TOKENS // TOK_DEV)
    route_turns = jax.random.permutation(jax.random.fold_in(key_list[1], 3), TOKENS // TOK_DEV)
    route = jax.vmap(lambda own, number: assign_block(jax.random.fold_in(key_list[1], 2), own, number, TOK_DEV, EXPERTS, 1, CAP, 2))(route_keys, route_turns).reshape((TOKENS, 1))
    gate_score = jnp.clip(jnp.exp(math.log(1.0) - 2.3025851 * jax.random.uniform(key_list[2], (TOKENS, 1), jnp.float32) ** steps_of(key_list[2], (TOKENS, 1), ((0, 64),), -0.2, 0.2)), 0.1, 1.0)
    w_gate = noise(key_list[3], (EXPERTS, D, FF), D ** -0.5, 0.09375, ((0, 64), (2, 16)))
    w_up = noise(key_list[4], (EXPERTS, D, FF), D ** -0.5, 0.09375, ((0, 64), (2, 16)))
    w_down = noise(key_list[5], (EXPERTS, FF, D), FF ** -0.5, 0.125, ((0, 64), (1, 16)))
    return dict(tokens=tokens, route=route, gate_score=gate_score, w_gate=w_gate, w_up=w_up, w_down=w_down)


def reference(tokens, route, gate_score, w_gate, w_up, w_down):
    total = tokens.shape[0]
    blocks = total // TOK_DEV
    target = route[:, 0].astype(jnp.int32)
    grid = target.reshape(blocks, TOK_DEV)
    onehot = (grid[:, :, None] == jnp.arange(EXPERTS, dtype=jnp.int32)[None, None, :]).astype(jnp.int32)
    earlier = jnp.cumsum(onehot, axis=1) - onehot
    rank = jnp.sum(earlier * onehot, axis=2).reshape(total).astype(jnp.int32)
    block_id = (jnp.arange(total, dtype=jnp.int32) // TOK_DEV).astype(jnp.int32)
    slot = (block_id * CAP + rank).astype(jnp.int32)
    table = jnp.zeros((EXPERTS, blocks * CAP), jnp.int32).at[target, slot].set(jnp.arange(total, dtype=jnp.int32))
    filled = jnp.zeros((EXPERTS, blocks * CAP), jnp.float32).at[target, slot].set(1.0)
    width = FF // N_BLK

    def run_expert(index):
        rows = tokens[table[index]] * filled[index][:, None].astype(jnp.bfloat16)
        gate = jnp.dot(rows, w_gate[index], preferred_element_type=jnp.float32)
        up = jnp.dot(rows, w_up[index], preferred_element_type=jnp.float32)
        hidden = (jax.nn.silu(gate) * up).astype(jnp.bfloat16)
        parts = jnp.einsum("sbf,bfd->bsd", hidden.reshape(-1, N_BLK, width).astype(jnp.float32), w_down[index].reshape(N_BLK, width, D).astype(jnp.float32))
        rounded = lax.optimization_barrier(parts.astype(jnp.bfloat16))
        return jnp.sum(rounded.astype(jnp.float32), axis=0).astype(jnp.bfloat16)

    outputs = lax.map(run_expert, jnp.arange(EXPERTS, dtype=jnp.int32))
    expert_out = outputs[target, slot]
    return (expert_out.astype(jnp.float32) * gate_score).astype(jnp.bfloat16)
```

```python
import functools

import jax
import jax.numpy as jnp
from jax import lax
from jax.experimental import pallas as pl
from jax.experimental.pallas import tpu as pltpu
from jax.sharding import Mesh
from jax.sharding import PartitionSpec as P

EXPERT = ("xl", "z", "core")
BLK = ("y", "xh")
MESH = pl.DeviceIdType.MESH
NZ, NY = 16, 8
EXPERTS, CAP = 64, 12
SLOTS = EXPERTS * CAP
HALF = SLOTS // 2
WIDE = 512
PIECES = 4


def remote(src, dst, send, recv, device):
    return pltpu.make_async_remote_copy(
        src_ref=src, dst_ref=dst, send_sem=send, recv_sem=recv, device_id=device, device_id_type=MESH
    )


def padded_halves(rows, groups):
    width = rows.shape[1]
    low = rows[:, :128]
    high = jnp.concatenate([rows[:, 128:], jnp.zeros((rows.shape[0], 256 - width), rows.dtype)], axis=1)
    return [part.reshape(groups, CAP // 4, 4, 128) for part in (low, high)]


def kernel(
    tok_ref, route_ref, score_ref, wg_ref, wu_ref, wd_ref, out_ref,
    sel, outgoing, arrived, rows, wg2, wu2, relay_g, relay_u, wd2, relay_d, acc, hidden, total,
    leaving, back,
    a_send, a_recv, r_send, r_recv, w_send, w_recv, d_send, d_recv, x_send, x_recv,
    ring_send, ring_recv, hid_send, hid_recv,
):
    xl, z, c = lax.axis_index("xl"), lax.axis_index("z"), lax.axis_index("core")
    y, xh = lax.axis_index("y"), lax.axis_index("xh")
    width = tok_ref.shape[0]
    right = (1 - xl, z, c, y, lax.rem(xh + xl, 2))
    left = (1 - xl, z, c, y, lax.rem(xh + 1 - xl, 2))
    up, down = lax.rem(y + 1, NY), lax.rem(y + NY - 1, NY)
    above, below = (xl, z, c, up, xh), (xl, z, c, down, xh)
    mixed = lax.rem(c + xh, 2)
    started = []

    def start(copy):
        copy.start()
        started.append(copy)

    barrier = pltpu.get_barrier_semaphore()

    def greet(device):
        pl.semaphore_signal(barrier, inc=1, device_id=device, device_id_type=MESH)

    def greet_plane(k, carry):
        zz = lax.rem(z + k, NZ)
        for a in range(2):
            for b in range(2):
                device = (lax.rem(xl + a, 2), zz, lax.rem(c + b, 2), y, c)
                if a == 0 and b == 0:
                    pl.when(k + mixed > 0)(functools.partial(greet, device))
                else:
                    greet(device)
            greet((lax.rem(xl + a, 2), zz, xh, y, 1 - c))
        return carry

    lax.fori_loop(0, NZ, greet_plane, 0)
    for k in range(1, NY):
        greet((xl, z, c, lax.rem(y + k, NY), xh))
    greet(right)
    greet(left)

    count = tok_ref.shape[1]
    target = route_ref[...]
    named = lax.broadcasted_iota(jnp.int32, (EXPERTS, count), 0) == target
    earlier = lax.broadcasted_iota(jnp.int32, (count, count), 0) < lax.broadcasted_iota(
        jnp.int32, (count, count), 1
    )
    before = jnp.dot(
        jnp.where(named, 1.0, 0.0).astype(jnp.bfloat16),
        jnp.where(earlier, 1.0, 0.0).astype(jnp.bfloat16),
        preferred_element_type=jnp.float32,
    )
    rank = jnp.sum(jnp.where(named, before, 0.0), axis=0, keepdims=True)
    slot = target.astype(jnp.float32) * CAP + rank
    place = lax.broadcasted_iota(jnp.int32, (SLOTS, count), 0).astype(jnp.float32)
    sel[...] = jnp.where(place == slot, 1.0, 0.0).astype(jnp.bfloat16)
    slotted = lax.dot_general(
        sel[...], tok_ref[...], (((1,), (1,)), ((), ())), preferred_element_type=jnp.float32
    ).astype(jnp.bfloat16)
    for h, part in enumerate(padded_halves(slotted, EXPERTS)):
        outgoing[h] = part

    pl.semaphore_wait(barrier, 2 * EXPERTS - EXPERTS // 2 + NY + mixed)

    mine = xl * NZ + z

    def far_first(k):
        return lax.rem(z + NZ // 2 + (1 - 2 * lax.rem(k, 2)) * ((k + 1) // 2) + NZ, NZ)

    def dispatch(k, carry):
        zz = far_first(k)
        for a in range(2):
            for b in range(2):
                xx, cc = lax.rem(xl + a, 2), lax.rem(c + b, 2)
                src = outgoing.at[:, (xx * NZ + zz) * 2 + cc]
                dst = arrived.at[xh, :, mine]
                away = remote(src, dst, a_send, a_recv, (xx, zz, cc, y, c))
                if a == 0 and b == 0:
                    pl.when((NZ - 1 - k) + mixed > 0)(away.start)

                    @pl.when((NZ - 1 - k) + mixed == 0)
                    def _():
                        pltpu.make_async_copy(src, dst, a_recv).start()
                else:
                    away.start()
        return carry

    lax.fori_loop(0, NZ, dispatch, 0)

    own_rows = pl.ds(pl.multiple_of(128 * xh, 128), 128)
    other_rows = pl.ds(pl.multiple_of(128 * (1 - xh), 128), 128)

    def columns_of(yy):
        return pl.ds(pl.multiple_of(128 * (7 * (yy // 2) + 3 * lax.rem(yy, 2)), 128), WIDE)

    kept = pltpu.make_async_copy(wd_ref.at[:, columns_of(y)], wd2.at[y, own_rows], d_recv.at[0])
    kept.start()
    spread = []
    for k in (4, 3, 5, 2, 6, 1, 7):
        yy = lax.rem(y + k, NY)
        copy = remote(
            wd_ref.at[:, columns_of(yy)], wd2.at[y, own_rows], d_send.at[k], d_recv.at[k], (xl, z, c, yy, xh)
        )
        start(copy)
        spread.append(k)

    part_rows = wg_ref.shape[0] // PIECES

    def weight_copies(p, hop):
        piece = pl.ds(part_rows * p, part_rows)
        g_src, u_src = (wg_ref, wu_ref) if hop == 0 else (relay_g, relay_u)
        g_dst, u_dst = (relay_g, relay_u) if hop == 0 else (wg2, wu2)
        return (
            remote(g_src.at[piece], g_dst.at[piece], w_send.at[hop, 0, p], w_recv.at[hop, 0, p], right),
            remote(u_src.at[piece], u_dst.at[piece], w_send.at[hop, 1, p], w_recv.at[hop, 1, p], left),
        )

    for p in range(PIECES):
        for copy in weight_copies(p, 0):
            start(copy)

    def relay_weights(p):
        for first, second in zip(weight_copies(p, 0), weight_copies(p, 1)):
            first.wait_recv()
            start(second)

    relay_weights(0)
    pltpu.make_async_copy(arrived, arrived, a_recv).wait()
    for s in range(2):
        for h in range(2):
            rows[y, s, h] = arrived[s, h].reshape(HALF, 128)

    def ring(view, subs, send, recv, work):
        def hop(origin, s, d, j):
            there = above if d == 0 else below
            return remote(view(origin, j), view(origin, j), send.at[d, s, j], recv.at[d, s, j], there)

        for j in range(subs):
            for d in range(2):
                start(hop(y, 0, d, j))
        work(0, y, None)
        for s in range(1, NY // 2 + 1):
            origins = (lax.rem(y - s + NY, NY), lax.rem(y + s, NY))
            for j in range(subs):
                for d in range(2):
                    whole_way = (j < subs // 2) == (d == 0)
                    if s == NY // 2 and not whole_way:
                        continue
                    hop(origins[d], s - 1, d, j).wait_recv()
                    if s < NY // 2 - 1 or (s == NY // 2 - 1 and whole_way):
                        start(hop(origins[d], s, d, j))
            if s < NY // 2:
                work(s, *origins)
            else:
                work(s, origins[0], None)

    def gate_up(origin, which, g_ref, u_ref):
        result = acc[which]
        for s in range(2):
            first_row = pl.ds(pl.multiple_of((2 * origin + s) * width, 32), width)
            values = jnp.concatenate([rows[origin, s, 0], rows[origin, s, 1]], axis=1)[:, :width]
            weights = jnp.concatenate([g_ref[first_row, :], u_ref[first_row, :]], axis=1)
            result = result + jnp.dot(values, weights, preferred_element_type=jnp.float32)
        acc[which] = result

    def first_work(s, one, two):
        if s == 0:
            acc[...] = jnp.zeros_like(acc)
        for origin in (one,) if two is None else (one, two):
            gate_up(origin, 0, wg_ref, wu_ref)
        if 1 <= s < PIECES:
            relay_weights(s)
        if s == 0:
            for k in range(NY):
                wait_spread(k)
        if s == 3:
            for p in range(NY):
                start(down_hop(p, 0))

    def wait_spread(k):
        source = lax.rem(y - k + NY, NY)
        dst = wd2.at[source, own_rows]
        pltpu.make_async_copy(dst, dst, d_recv.at[k]).wait()

    def down_hop(p, hop):
        there = right if p % 2 == 0 else left
        origin_xh = lax.rem(xh + 1 - xl, 2) if p % 2 == 0 else lax.rem(xh + xl, 2)
        if hop == 0:
            return remote(wd2.at[p, own_rows], relay_d.at[p], x_send.at[0, p], x_recv.at[0, p], there)
        there_rows = pl.ds(pl.multiple_of(128 * origin_xh, 128), 128)
        return remote(relay_d.at[p], wd2.at[p, there_rows], x_send.at[1, p], x_recv.at[1, p], there)

    ring(
        lambda origin, j: rows.at[origin, j // 2, j % 2], 4, ring_send, ring_recv, first_work
    )

    for p in range(PIECES):
        for copy in weight_copies(p, 1):
            copy.wait_recv()

    def other_units(k, carry):
        gate_up(k, 1, wg2, wu2)
        return carry

    lax.fori_loop(0, NY, other_units, 0)
    for which, plane in ((0, xh), (1, 1 - xh)):
        gate, value = acc[which, :, :128], acc[which, :, 128:]
        hidden[y, plane] = (gate / (1.0 + jnp.exp(-gate)) * value).astype(jnp.bfloat16)

    def down_relay(p):
        down_hop(p, 0).wait_recv()
        start(down_hop(p, 1))

    def project(origin):
        values = jnp.concatenate([hidden[origin, 0], hidden[origin, 1]], axis=1)
        total[...] += jnp.dot(values, wd2[origin], preferred_element_type=jnp.float32)

    def second_work(s, one, two):
        if s < 4:
            down_relay(2 * s)
            down_relay(2 * s + 1)

    ring(
        lambda origin, j: hidden.at[origin, j // 2, pl.ds(HALF // 2 * (j % 2), HALF // 2)],
        4, hid_send, hid_recv, second_work,
    )
    for p in range(NY):
        dst = wd2.at[p, other_rows]
        pltpu.make_async_copy(dst, dst, x_recv.at[1, p]).wait()
    total[...] = jnp.zeros_like(total)

    def projections(k, carry):
        project(k)
        return carry

    lax.fori_loop(0, NY, projections, 0)
    summed = total[...]
    summed = jnp.where(lax.rem(y, 2) == 1, summed[:, WIDE - 2 * width :], summed[:, : 2 * width])
    for s in range(2):
        share = summed[:, s * width : (s + 1) * width].astype(jnp.bfloat16)
        for h, part in enumerate(padded_halves(share, EXPERTS // 2)):
            leaving[s, h] = part

    expert = mine * 2 + c

    def give_back(k, carry):
        zz = far_first(k)
        for a in range(2):
            for b in range(2):
                xx, there = lax.rem(xl + a, 2), lax.rem(xh + b, 2)
                src = leaving.at[there, :, xx * NZ + zz]
                dst = back.at[:, expert]
                away = remote(src, dst, r_send, r_recv, (xx, zz, xh, y, there))
                if a == 0 and b == 0:
                    pl.when((NZ - 1 - k) + mixed > 0)(away.start)

                    @pl.when((NZ - 1 - k) + mixed == 0)
                    def _():
                        pltpu.make_async_copy(src, dst, r_recv).start()
                else:
                    away.start()
        return carry

    lax.fori_loop(0, NZ, give_back, 0)
    pltpu.make_async_copy(back, back, r_recv).wait()
    returned = jnp.concatenate([back[h].reshape(SLOTS, 128) for h in range(2)], axis=1)[:, :width]
    picked = lax.dot_general(
        returned, sel[...], (((0,), (0,)), ((), ())), preferred_element_type=jnp.float32
    )
    out_ref[...] = (picked * score_ref[...]).astype(jnp.bfloat16)

    for copy in started:
        copy.wait_send()
    for sem in (a_send, r_send):

        @pl.when(mixed == 1)
        def _():
            pltpu.make_async_copy(outgoing, outgoing, sem).wait()

        @pl.when(mixed == 0)
        def _():
            most = outgoing.at[:, pl.ds(0, EXPERTS - 1)]
            pltpu.make_async_copy(most, most, sem).wait()


def per_device(tokens, route, gate_score, w_gate, w_up, w_down):
    count, width = tokens.shape
    features, units = w_gate.shape[1:]
    bf16, f32 = jnp.bfloat16, jnp.float32
    dma = pltpu.SemaphoreType.DMA
    result = pl.pallas_call(
        kernel,
        out_shape=jax.ShapeDtypeStruct((width, count), bf16),
        in_specs=[pl.BlockSpec(memory_space=pltpu.VMEM)] * 6,
        out_specs=pl.BlockSpec(memory_space=pltpu.VMEM),
        scratch_shapes=[
            pltpu.VMEM((SLOTS, count), bf16),
            pltpu.VMEM((2, EXPERTS, CAP // 4, 4, 128), bf16),
            pltpu.VMEM((2, 2, EXPERTS // 2, CAP // 4, 4, 128), bf16),
            pltpu.VMEM((NY, 2, 2, HALF, 128), bf16),
            pltpu.VMEM((features, units), bf16),
            pltpu.VMEM((features, units), bf16),
            pltpu.VMEM((features, units), bf16),
            pltpu.VMEM((features, units), bf16),
            pltpu.VMEM((NY, 2 * units, WIDE), bf16),
            pltpu.VMEM((NY, units, WIDE), bf16),
            pltpu.VMEM((2, HALF, 2 * units), f32),
            pltpu.VMEM((NY, 2, HALF, units), bf16),
            pltpu.VMEM((HALF, WIDE), f32),
            pltpu.VMEM((2, 2, EXPERTS // 2, CAP // 4, 4, 128), bf16),
            pltpu.VMEM((2, EXPERTS, CAP // 4, 4, 128), bf16),
            dma, dma, dma, dma,
            dma((2, 2, PIECES)), dma((2, 2, PIECES)),
            dma((NY,)), dma((NY,)),
            dma((2, NY)), dma((2, NY)),
            dma((2, NY // 2, 4)), dma((2, NY // 2, 4)),
            dma((2, NY // 2, 4)), dma((2, NY // 2, 4)),
        ],
        compiler_params=pltpu.CompilerParams(collective_id=0, has_side_effects=True),
        name="experts",
    )(tokens.T, route.T, gate_score.T, w_gate[0], w_up[0], w_down[0])
    return result.T


def solution(mesh):
    split = Mesh(mesh.devices.reshape(2, NZ, 2, NY, 2), EXPERT + BLK)
    return jax.shard_map(
        per_device,
        mesh=split,
        in_specs=(
            P(EXPERT, BLK),
            P(EXPERT, None),
            P(EXPERT, None),
            P(EXPERT, None, BLK),
            P(EXPERT, None, BLK),
            P(EXPERT, BLK, None),
        ),
        out_specs=P(EXPERT, BLK),
        check_vma=False,
    )
```

```python
import functools

import jax
import jax.numpy as jnp
from jax import lax
from jax.experimental import pallas as pl
from jax.experimental.pallas import tpu as pltpu
from jax.sharding import Mesh
from jax.sharding import PartitionSpec as P

EXPERT = ("xl", "z", "core")
BLK = ("y", "xh")
MESH = pl.DeviceIdType.MESH
NZ, NY = 16, 8
EXPERTS, CAP = 64, 12
SLOTS = EXPERTS * CAP
HALF = SLOTS // 2
WIDE = 512
PIECES = 8
EARLY = 3
PACK = 4


def remote(src, dst, send, recv, device):
    return pltpu.make_async_remote_copy(
        src_ref=src, dst_ref=dst, send_sem=send, recv_sem=recv, device_id=device, device_id_type=MESH
    )


def padded_halves(rows, groups):
    width = rows.shape[1]
    low = rows[:, :128]
    high = jnp.concatenate([rows[:, 128:], jnp.zeros((rows.shape[0], 256 - width), rows.dtype)], axis=1)
    return [part.reshape(groups, CAP // 4, 4, 128) for part in (low, high)]


def kernel(
    tok_ref, route_ref, score_ref, wg_ref, wu_ref, wd_ref, out_ref,
    sel, outgoing, arrived, low, high, wg, wu, wg2, wu2, wd2, acc, hidden, total, leaving, back,
    a_send, a_recv, r_send, r_recv, w_load, w_send, w_recv, d_send, d_recv, x_send, x_recv,
    ring_send, ring_recv, hid_send, hid_recv, round_sem,
):
    xl, z, c = lax.axis_index("xl"), lax.axis_index("z"), lax.axis_index("core")
    y, xh = lax.axis_index("y"), lax.axis_index("xh")
    width = tok_ref.shape[0]
    opposite = (xl, z, c, y, 1 - xh)
    up, down = lax.rem(y + 1, NY), lax.rem(y + NY - 1, NY)
    above, below = (xl, z, c, up, xh), (xl, z, c, down, xh)
    mixed = lax.rem(c + xh, 2)
    started = []

    def start(copy):
        copy.start()
        started.append(copy)

    loads = [
        pltpu.make_async_copy(wg_ref, wg, w_load.at[0]),
        pltpu.make_async_copy(wu_ref, wu, w_load.at[1]),
    ]
    for copy in loads:
        copy.start()

    barrier = pltpu.get_barrier_semaphore()
    ahead, behind = (xl, lax.rem(z + 1, NZ), c, y, xh), (xl, lax.rem(z + NZ - 1, NZ), c, y, xh)
    near = [ahead, behind]
    for k in range(1, 8):
        near.append((lax.rem(xl + k // 4, 2), z, lax.rem(c + k // 2 % 2, 2), y, lax.rem(xh + k % 2, 2)))
    for k in range(1, NY):
        near.append((xl, z, c, lax.rem(y + k, NY), xh))
    for device in near:
        pl.semaphore_signal(barrier, inc=1, device_id=device, device_id_type=MESH)

    count = tok_ref.shape[1]
    target = route_ref[...]
    named = lax.broadcasted_iota(jnp.int32, (EXPERTS, count), 0) == target
    earlier = lax.broadcasted_iota(jnp.int32, (count, count), 0) < lax.broadcasted_iota(
        jnp.int32, (count, count), 1
    )
    before = jnp.dot(
        jnp.where(named, 1.0, 0.0).astype(jnp.bfloat16),
        jnp.where(earlier, 1.0, 0.0).astype(jnp.bfloat16),
        preferred_element_type=jnp.float32,
    )
    rank = jnp.sum(jnp.where(named, before, 0.0), axis=0, keepdims=True)
    slot = target.astype(jnp.float32) * CAP + rank
    place = lax.broadcasted_iota(jnp.int32, (SLOTS, count), 0).astype(jnp.float32)
    sel[...] = jnp.where(place == slot, 1.0, 0.0).astype(jnp.bfloat16)
    slotted = lax.dot_general(
        sel[...], tok_ref[...], (((1,), (1,)), ((), ())), preferred_element_type=jnp.float32
    ).astype(jnp.bfloat16)
    for h, part in enumerate(padded_halves(slotted, EXPERTS)):
        outgoing[h] = part

    pl.semaphore_wait(barrier, len(near))

    own_rows = pl.ds(pl.multiple_of(128 * xh, 128), 128)
    other_rows = pl.ds(pl.multiple_of(128 * (1 - xh), 128), 128)

    def columns_of(yy):
        return pl.ds(pl.multiple_of(128 * (7 * (yy // 2) + 3 * lax.rem(yy, 2)), 128), WIDE)

    kept = pltpu.make_async_copy(wd_ref.at[:, columns_of(y)], wd2.at[y, own_rows], d_recv.at[0])
    kept.start()
    for k in (4, 3, 5, 2, 6, 1, 7):
        yy = lax.rem(y + k, NY)
        copy = remote(
            wd_ref.at[:, columns_of(yy)], wd2.at[y, own_rows], d_send.at[k], d_recv.at[k], (xl, z, c, yy, xh)
        )
        start(copy)

    part_rows = wg_ref.shape[0] // PIECES

    def weight_copies(p):
        piece = pl.ds(part_rows * p, part_rows)
        return (
            remote(wg_ref.at[piece], wg2.at[piece], w_send.at[0, p], w_recv.at[0, p], opposite),
            remote(wu_ref.at[piece], wu2.at[piece], w_send.at[1, p], w_recv.at[1, p], opposite),
        )

    for p in range(EARLY):
        start(weight_copies(p)[0])

    mine = xl * NZ + z

    def dispatch(zz, here):
        for a in range(2):
            for b in range(2):
                xx, cc = lax.rem(xl + a, 2), lax.rem(c + b, 2)
                src = outgoing.at[:, (xx * NZ + zz) * 2 + cc]
                dst = arrived.at[xh, :, mine]
                away = remote(src, dst, a_send, a_recv, (xx, zz, cc, y, c))
                if here and a == 0 and b == 0:
                    pl.when(mixed == 1)(away.start)

                    @pl.when(mixed == 0)
                    def _():
                        pltpu.make_async_copy(src, dst, a_recv).start()
                else:
                    away.start()

    dispatch(z, True)

    def next_round(r, carry):
        for device in (ahead, behind):
            pl.semaphore_signal(round_sem.at[r], inc=1, device_id=device, device_id_type=MESH)
        pl.semaphore_wait(round_sem.at[r], 2)
        dispatch(lax.rem(z + r + 1, NZ), False)
        dispatch(lax.rem(z + NZ - 1 - r, NZ), False)
        return carry

    lax.fori_loop(0, NZ // 2 - 1, next_round, 0)
    last = NZ // 2 - 1
    for device in (ahead, behind):
        pl.semaphore_signal(round_sem.at[last], inc=1, device_id=device, device_id_type=MESH)
    pl.semaphore_wait(round_sem.at[last], 2)
    dispatch(lax.rem(z + NZ // 2, NZ), False)

    for p in range(PIECES):
        for which, copy in enumerate(weight_copies(p)):
            if which == 1 or p >= EARLY:
                start(copy)

    def far_first(k):
        return lax.rem(z + NZ // 2 + (1 - 2 * lax.rem(k, 2)) * ((k + 1) // 2) + NZ, NZ)

    pltpu.make_async_copy(arrived, arrived, a_recv).wait()
    block = HALF // PACK
    rest = width - 128
    for s in range(2):
        low[y, s] = arrived[s, 0].reshape(HALF, 128)
        upper = arrived[s, 1].reshape(HALF, 128)
        high[y, s] = jnp.concatenate(
            [upper[block * i : block * (i + 1), :rest] for i in range(PACK)], axis=1
        )

    def ring(view, subs, send, recv, work):
        def hop(origin, s, d, j):
            there = above if d == 0 else below
            return remote(view(origin, j), view(origin, j), send.at[d, s, j], recv.at[d, s, j], there)

        for j in range(subs):
            for d in range(2):
                start(hop(y, 0, d, j))
        work(0, y, None)
        for s in range(1, NY // 2 + 1):
            origins = (lax.rem(y - s + NY, NY), lax.rem(y + s, NY))
            for j in range(subs):
                for d in range(2):
                    whole_way = (j < subs // 2) == (d == 0)
                    if s == NY // 2 and not whole_way:
                        continue
                    hop(origins[d], s - 1, d, j).wait_recv()
                    if s < NY // 2 - 1 or (s == NY // 2 - 1 and whole_way):
                        start(hop(origins[d], s, d, j))
            if s < NY // 2:
                work(s, *origins)
            else:
                work(s, origins[0], None)

    def gate_up(origin, which, g_ref, u_ref):
        result = acc[which]
        for s in range(2):
            first_row = pl.ds(pl.multiple_of((2 * origin + s) * width, 32), width)
            packed = high[origin, s]
            upper = jnp.concatenate([packed[:, rest * i : rest * (i + 1)] for i in range(PACK)], axis=0)
            values = jnp.concatenate([low[origin, s], upper], axis=1)
            weights = jnp.concatenate([g_ref[first_row, :], u_ref[first_row, :]], axis=1)
            result = result + jnp.dot(values, weights, preferred_element_type=jnp.float32)
        acc[which] = result

    def first_work(s, one, two):
        if s == 0:
            acc[...] = jnp.zeros_like(acc)
            for copy in loads:
                copy.wait()
        fresh = (one,) if two is None else (one, two)
        for origin in fresh:
            gate_up(origin, 0, wg, wu)
        if s == 1:
            for k in range(NY):
                wait_spread(k)
            for p in range(NY):
                start(across(p))
        if s == NY // 2 - 1:
            for p in range(PIECES):
                for copy in weight_copies(p):
                    copy.wait_recv()
            lax.fori_loop(NY // 2 + 2, NY + NY // 2 - 1, other_units, 0)
        if s == NY // 2:
            lax.fori_loop(NY // 2 - 1, NY // 2 + 2, other_units, 0)

    def other_units(k, carry):
        gate_up(lax.rem(y + k, NY), 1, wg2, wu2)
        return carry

    def wait_spread(k):
        source = lax.rem(y - k + NY, NY)
        dst = wd2.at[source, own_rows]
        pltpu.make_async_copy(dst, dst, d_recv.at[k]).wait()

    def across(p):
        return remote(wd2.at[p, own_rows], wd2.at[p, own_rows], x_send.at[p], x_recv.at[p], opposite)

    ring(
        lambda origin, j: (low, high)[j % 2].at[origin, j // 2], 4, ring_send, ring_recv, first_work
    )

    for which, plane in ((0, xh), (1, 1 - xh)):
        gate, value = acc[which, :, :128], acc[which, :, 128:]
        hidden[y, plane] = (gate / (1.0 + jnp.exp(-gate)) * value).astype(jnp.bfloat16)

    def project(origin):
        values = jnp.concatenate([hidden[origin, 0], hidden[origin, 1]], axis=1)
        total[...] += jnp.dot(values, wd2[origin], preferred_element_type=jnp.float32)

    def projections(k, carry):
        project(lax.rem(y + k, NY))
        return carry

    def second_work(s, one, two):
        if s == 0:
            total[...] = jnp.zeros_like(total)
        if s == NY // 2 - 1:
            for p in range(NY):
                dst = wd2.at[p, other_rows]
                pltpu.make_async_copy(dst, dst, x_recv.at[p]).wait()
            lax.fori_loop(NY // 2 + 2, NY + NY // 2 - 1, projections, 0)
        if s == NY // 2:
            lax.fori_loop(NY // 2 - 1, NY // 2 + 2, projections, 0)

    ring(
        lambda origin, j: hidden.at[origin, j // 2, pl.ds(HALF // 2 * (j % 2), HALF // 2)],
        4, hid_send, hid_recv, second_work,
    )
    summed = total[...]
    summed = jnp.where(lax.rem(y, 2) == 1, summed[:, WIDE - 2 * width :], summed[:, : 2 * width])
    for s in range(2):
        share = summed[:, s * width : (s + 1) * width].astype(jnp.bfloat16)
        for h, part in enumerate(padded_halves(share, EXPERTS // 2)):
            leaving[s, h] = part

    expert = mine * 2 + c

    def give_back(k, carry):
        zz = far_first(k)
        for a in range(2):
            for b in range(2):
                xx, there = lax.rem(xl + a, 2), lax.rem(xh + b, 2)
                src = leaving.at[there, :, xx * NZ + zz]
                dst = back.at[:, expert]
                away = remote(src, dst, r_send, r_recv, (xx, zz, xh, y, there))
                if a == 0 and b == 0:
                    pl.when((NZ - 1 - k) + mixed > 0)(away.start)

                    @pl.when((NZ - 1 - k) + mixed == 0)
                    def _():
                        pltpu.make_async_copy(src, dst, r_recv).start()
                else:
                    away.start()
        return carry

    lax.fori_loop(0, NZ, give_back, 0)
    pltpu.make_async_copy(back, back, r_recv).wait()
    returned = jnp.concatenate([back[h].reshape(SLOTS, 128) for h in range(2)], axis=1)[:, :width]
    picked = lax.dot_general(
        returned, sel[...], (((0,), (0,)), ((), ())), preferred_element_type=jnp.float32
    )
    out_ref[...] = (picked * score_ref[...]).astype(jnp.bfloat16)

    for copy in started:
        copy.wait_send()
    for sem in (a_send, r_send):

        @pl.when(mixed == 1)
        def _():
            pltpu.make_async_copy(outgoing, outgoing, sem).wait()

        @pl.when(mixed == 0)
        def _():
            most = outgoing.at[:, pl.ds(0, EXPERTS - 1)]
            pltpu.make_async_copy(most, most, sem).wait()


def per_device(tokens, route, gate_score, w_gate, w_up, w_down):
    count, width = tokens.shape
    features, units = w_gate.shape[1:]
    bf16, f32 = jnp.bfloat16, jnp.float32
    dma = pltpu.SemaphoreType.DMA
    result = pl.pallas_call(
        kernel,
        out_shape=jax.ShapeDtypeStruct((width, count), bf16),
        in_specs=[pl.BlockSpec(memory_space=pltpu.VMEM)] * 3 + [pl.BlockSpec(memory_space=pl.ANY)] * 3,
        out_specs=pl.BlockSpec(memory_space=pltpu.VMEM),
        scratch_shapes=[
            pltpu.VMEM((SLOTS, count), bf16),
            pltpu.VMEM((2, EXPERTS, CAP // 4, 4, 128), bf16),
            pltpu.VMEM((2, 2, EXPERTS // 2, CAP // 4, 4, 128), bf16),
            pltpu.VMEM((NY, 2, HALF, 128), bf16),
            pltpu.VMEM((NY, 2, HALF // PACK, PACK * (width - 128)), bf16),
            pltpu.VMEM((features, units), bf16),
            pltpu.VMEM((features, units), bf16),
            pltpu.VMEM((features, units), bf16),
            pltpu.VMEM((features, units), bf16),
            pltpu.VMEM((NY, 2 * units, WIDE), bf16),
            pltpu.VMEM((2, HALF, 2 * units), f32),
            pltpu.VMEM((NY, 2, HALF, units), bf16),
            pltpu.VMEM((HALF, WIDE), f32),
            pltpu.VMEM((2, 2, EXPERTS // 2, CAP // 4, 4, 128), bf16),
            pltpu.VMEM((2, EXPERTS, CAP // 4, 4, 128), bf16),
            dma, dma, dma, dma,
            dma((2,)), dma((2, PIECES)), dma((2, PIECES)),
            dma((NY,)), dma((NY,)),
            dma((NY,)), dma((NY,)),
            dma((2, NY // 2, 4)), dma((2, NY // 2, 4)),
            dma((2, NY // 2, 4)), dma((2, NY // 2, 4)),
            pltpu.SemaphoreType.REGULAR((NZ // 2,)),
        ],
        compiler_params=pltpu.CompilerParams(collective_id=0, has_side_effects=True),
        name="experts",
    )(tokens.T, route.T, gate_score.T, w_gate[0], w_up[0], w_down[0])
    return result.T


def solution(mesh):
    split = Mesh(mesh.devices.reshape(2, NZ, 2, NY, 2), EXPERT + BLK)
    return jax.shard_map(
        per_device,
        mesh=split,
        in_specs=(
            P(EXPERT, BLK),
            P(EXPERT, None),
            P(EXPERT, None),
            P(EXPERT, None, BLK),
            P(EXPERT, None, BLK),
            P(EXPERT, BLK, None),
        ),
        out_specs=P(EXPERT, BLK),
        check_vma=False,
    )
```

```python
import functools

import jax
import jax.numpy as jnp
from jax import lax
from jax.experimental import pallas as pl
from jax.experimental.pallas import tpu as pltpu
from jax.sharding import Mesh
from jax.sharding import PartitionSpec as P

EXPERT = ("xl", "z", "core")
BLK = ("y", "xh")
MESH = pl.DeviceIdType.MESH
NZ, NY = 16, 8
EXPERTS, CAP = 64, 12
SLOTS = EXPERTS * CAP
HALF = SLOTS // 2
WIDE = 512
PIECES = 8
EARLY = 3
PACK = 4


def remote(src, dst, send, recv, device):
    return pltpu.make_async_remote_copy(
        src_ref=src, dst_ref=dst, send_sem=send, recv_sem=recv, device_id=device, device_id_type=MESH
    )


def padded_halves(rows, groups):
    width = rows.shape[1]
    low = rows[:, :128]
    high = jnp.concatenate([rows[:, 128:], jnp.zeros((rows.shape[0], 256 - width), rows.dtype)], axis=1)
    return [part.reshape(groups, CAP // 4, 4, 128) for part in (low, high)]


def kernel(
    tok_ref, route_ref, score_ref, wg_ref, wu_ref, wd_ref, out_ref,
    sel, outgoing, arrived, low, high, wg, wu, wg2, wu2, wd2, acc, hidden, total, leaving, back,
    a_send, a_recv, r_send, r_recv, w_load, w_send, w_recv, d_send, d_recv, x_send, x_recv,
    ring_send, ring_recv, hid_send, hid_recv, round_sem,
):
    xl, z, c = lax.axis_index("xl"), lax.axis_index("z"), lax.axis_index("core")
    y, xh = lax.axis_index("y"), lax.axis_index("xh")
    width = tok_ref.shape[0]
    opposite = (xl, z, c, y, 1 - xh)
    up, down = lax.rem(y + 1, NY), lax.rem(y + NY - 1, NY)
    above, below = (xl, z, c, up, xh), (xl, z, c, down, xh)
    mixed = lax.rem(c + xh, 2)
    started = []

    def start(copy):
        copy.start()
        started.append(copy)

    loads = [
        pltpu.make_async_copy(wg_ref, wg, w_load.at[0]),
        pltpu.make_async_copy(wu_ref, wu, w_load.at[1]),
    ]
    for copy in loads:
        copy.start()

    barrier = pltpu.get_barrier_semaphore()
    ahead, behind = (xl, lax.rem(z + 1, NZ), c, y, xh), (xl, lax.rem(z + NZ - 1, NZ), c, y, xh)
    near = [ahead, behind]
    for k in range(1, 8):
        near.append((lax.rem(xl + k // 4, 2), z, lax.rem(c + k // 2 % 2, 2), y, lax.rem(xh + k % 2, 2)))
    for k in range(1, NY):
        near.append((xl, z, c, lax.rem(y + k, NY), xh))
    for device in near:
        pl.semaphore_signal(barrier, inc=1, device_id=device, device_id_type=MESH)

    count = tok_ref.shape[1]
    target = route_ref[...]
    named = lax.broadcasted_iota(jnp.int32, (EXPERTS, count), 0) == target
    earlier = lax.broadcasted_iota(jnp.int32, (count, count), 0) < lax.broadcasted_iota(
        jnp.int32, (count, count), 1
    )
    before = jnp.dot(
        jnp.where(named, 1.0, 0.0).astype(jnp.bfloat16),
        jnp.where(earlier, 1.0, 0.0).astype(jnp.bfloat16),
        preferred_element_type=jnp.float32,
    )
    rank = jnp.sum(jnp.where(named, before, 0.0), axis=0, keepdims=True)
    slot = target.astype(jnp.float32) * CAP + rank
    place = lax.broadcasted_iota(jnp.int32, (SLOTS, count), 0).astype(jnp.float32)
    sel[...] = jnp.where(place == slot, 1.0, 0.0).astype(jnp.bfloat16)
    slotted = lax.dot_general(
        sel[...], tok_ref[...], (((1,), (1,)), ((), ())), preferred_element_type=jnp.float32
    ).astype(jnp.bfloat16)
    for h, part in enumerate(padded_halves(slotted, EXPERTS)):
        outgoing[h] = part

    pl.semaphore_wait(barrier, len(near))

    own_rows = pl.ds(pl.multiple_of(128 * xh, 128), 128)
    other_rows = pl.ds(pl.multiple_of(128 * (1 - xh), 128), 128)

    def columns_of(yy):
        return pl.ds(pl.multiple_of(128 * (7 * (yy // 2) + 3 * lax.rem(yy, 2)), 128), WIDE)

    kept = pltpu.make_async_copy(wd_ref.at[:, columns_of(y)], wd2.at[y, own_rows], d_recv.at[0])
    kept.start()
    for k in (4, 3, 5, 2, 6, 1, 7):
        yy = lax.rem(y + k, NY)
        copy = remote(
            wd_ref.at[:, columns_of(yy)], wd2.at[y, own_rows], d_send.at[k], d_recv.at[k], (xl, z, c, yy, xh)
        )
        start(copy)

    part_rows = wg_ref.shape[0] // PIECES

    def weight_copies(p):
        piece = pl.ds(part_rows * p, part_rows)
        return (
            remote(wg_ref.at[piece], wg2.at[piece], w_send.at[0, p], w_recv.at[0, p], opposite),
            remote(wu_ref.at[piece], wu2.at[piece], w_send.at[1, p], w_recv.at[1, p], opposite),
        )

    for p in range(EARLY):
        start(weight_copies(p)[0])

    mine = xl * NZ + z

    def dispatch(zz, here):
        for a in range(2):
            for b in range(2):
                xx, cc = lax.rem(xl + a, 2), lax.rem(c + b, 2)
                src = outgoing.at[:, (xx * NZ + zz) * 2 + cc]
                dst = arrived.at[xh, :, mine]
                away = remote(src, dst, a_send, a_recv, (xx, zz, cc, y, c))
                if here and a == 0 and b == 0:
                    pl.when(mixed == 1)(away.start)

                    @pl.when(mixed == 0)
                    def _():
                        pltpu.make_async_copy(src, dst, a_recv).start()
                else:
                    away.start()

    dispatch(z, True)

    def next_round(r, carry):
        for device in (ahead, behind):
            pl.semaphore_signal(round_sem.at[r], inc=1, device_id=device, device_id_type=MESH)
        pl.semaphore_wait(round_sem.at[r], 2)
        dispatch(lax.rem(z + r + 1, NZ), False)
        dispatch(lax.rem(z + NZ - 1 - r, NZ), False)
        return carry

    lax.fori_loop(0, NZ // 2 - 1, next_round, 0)
    last = NZ // 2 - 1
    for device in (ahead, behind):
        pl.semaphore_signal(round_sem.at[last], inc=1, device_id=device, device_id_type=MESH)
    pl.semaphore_wait(round_sem.at[last], 2)
    dispatch(lax.rem(z + NZ // 2, NZ), False)

    for p in range(PIECES):
        for which, copy in enumerate(weight_copies(p)):
            if which == 1 or p >= EARLY:
                start(copy)

    def far_first(k):
        return lax.rem(z + NZ // 2 + (1 - 2 * lax.rem(k, 2)) * ((k + 1) // 2) + NZ, NZ)

    pltpu.make_async_copy(arrived, arrived, a_recv).wait()
    block = HALF // PACK
    rest = width - 128

    def plain_rows(j):
        half = arrived[j // 2, j % 2].reshape(HALF, 128)
        if j % 2 == 0:
            low[y, j // 2] = half
        else:
            high[y, j // 2] = jnp.concatenate(
                [half[block * i : block * (i + 1), :rest] for i in range(PACK)], axis=1
            )

    def ring(view, subs, send, recv, work, prepare=None):
        def hop(origin, s, d, j):
            there = above if d == 0 else below
            return remote(view(origin, j), view(origin, j), send.at[d, s, j], recv.at[d, s, j], there)

        for j in range(subs):
            if prepare is not None:
                prepare(j)
            for d in range(2):
                start(hop(y, 0, d, j))
        work(0, y, None)
        for s in range(1, NY // 2 + 1):
            origins = (lax.rem(y - s + NY, NY), lax.rem(y + s, NY))
            for j in range(subs):
                for d in range(2):
                    whole_way = (j < subs // 2) == (d == 0)
                    if s == NY // 2 and not whole_way:
                        continue
                    hop(origins[d], s - 1, d, j).wait_recv()
                    if s < NY // 2 - 1 or (s == NY // 2 - 1 and whole_way):
                        start(hop(origins[d], s, d, j))
            if s < NY // 2:
                work(s, *origins)
            else:
                work(s, origins[0], None)

    def gate_up(origin, which, g_ref, u_ref):
        result = acc[which]
        for s in range(2):
            first_row = pl.ds(pl.multiple_of((2 * origin + s) * width, 32), width)
            packed = high[origin, s]
            upper = jnp.concatenate([packed[:, rest * i : rest * (i + 1)] for i in range(PACK)], axis=0)
            values = jnp.concatenate([low[origin, s], upper], axis=1)
            weights = jnp.concatenate([g_ref[first_row, :], u_ref[first_row, :]], axis=1)
            result = result + jnp.dot(values, weights, preferred_element_type=jnp.float32)
        acc[which] = result

    def first_work(s, one, two):
        if s == 0:
            acc[...] = jnp.zeros_like(acc)
            for copy in loads:
                copy.wait()
        fresh = (one,) if two is None else (one, two)
        for origin in fresh:
            gate_up(origin, 0, wg, wu)
        if s == 1:
            for k in range(NY):
                wait_spread(k)
            for p in range(NY):
                start(across(p))
        if s == NY // 2 - 1:
            for p in range(PIECES):
                for copy in weight_copies(p):
                    copy.wait_recv()
            lax.fori_loop(NY // 2 + 2, NY + NY // 2 - 1, other_units, 0)
        if s == NY // 2:
            lax.fori_loop(NY // 2 - 1, NY // 2 + 2, other_units, 0)

    def other_units(k, carry):
        gate_up(lax.rem(y + k, NY), 1, wg2, wu2)
        return carry

    def wait_spread(k):
        source = lax.rem(y - k + NY, NY)
        dst = wd2.at[source, own_rows]
        pltpu.make_async_copy(dst, dst, d_recv.at[k]).wait()

    def across(p):
        return remote(wd2.at[p, own_rows], wd2.at[p, own_rows], x_send.at[p], x_recv.at[p], opposite)

    ring(
        lambda origin, j: (low, high)[j % 2].at[origin, j // 2], 4, ring_send, ring_recv, first_work,
        plain_rows,
    )

    for which, plane in ((0, xh), (1, 1 - xh)):
        gate, value = acc[which, :, :128], acc[which, :, 128:]
        hidden[y, plane] = (gate / (1.0 + jnp.exp(-gate)) * value).astype(jnp.bfloat16)

    def project(origin):
        values = jnp.concatenate([hidden[origin, 0], hidden[origin, 1]], axis=1)
        total[...] += jnp.dot(values, wd2[origin], preferred_element_type=jnp.float32)

    def projections(k, carry):
        project(lax.rem(y + k, NY))
        return carry

    def second_work(s, one, two):
        if s == 0:
            total[...] = jnp.zeros_like(total)
        if s == NY // 2 - 1:
            for p in range(NY):
                dst = wd2.at[p, other_rows]
                pltpu.make_async_copy(dst, dst, x_recv.at[p]).wait()
            lax.fori_loop(NY // 2 + 2, NY + NY // 2 - 1, projections, 0)
        if s == NY // 2:
            lax.fori_loop(NY // 2 - 1, NY // 2 + 2, projections, 0)

    ring(
        lambda origin, j: hidden.at[origin, j // 2, pl.ds(HALF // 2 * (j % 2), HALF // 2)],
        4, hid_send, hid_recv, second_work,
    )
    summed = total[...]
    summed = jnp.where(lax.rem(y, 2) == 1, summed[:, WIDE - 2 * width :], summed[:, : 2 * width])
    for s in range(2):
        share = summed[:, s * width : (s + 1) * width].astype(jnp.bfloat16)
        for h, part in enumerate(padded_halves(share, EXPERTS // 2)):
            leaving[s, h] = part

    expert = mine * 2 + c

    def give_back(k, carry):
        zz = far_first(k)
        for a in range(2):
            for b in range(2):
                xx, there = lax.rem(xl + a, 2), lax.rem(xh + b, 2)
                src = leaving.at[there, :, xx * NZ + zz]
                dst = back.at[:, expert]
                away = remote(src, dst, r_send, r_recv, (xx, zz, xh, y, there))
                if a == 0 and b == 0:
                    pl.when((NZ - 1 - k) + mixed > 0)(away.start)

                    @pl.when((NZ - 1 - k) + mixed == 0)
                    def _():
                        pltpu.make_async_copy(src, dst, r_recv).start()
                else:
                    away.start()
        return carry

    lax.fori_loop(0, NZ, give_back, 0)
    pltpu.make_async_copy(back, back, r_recv).wait()
    returned = jnp.concatenate([back[h].reshape(SLOTS, 128) for h in range(2)], axis=1)[:, :width]
    picked = lax.dot_general(
        returned, sel[...], (((0,), (0,)), ((), ())), preferred_element_type=jnp.float32
    )
    out_ref[...] = (picked * score_ref[...]).astype(jnp.bfloat16)

    for copy in started:
        copy.wait_send()
    for sem in (a_send, r_send):

        @pl.when(mixed == 1)
        def _():
            pltpu.make_async_copy(outgoing, outgoing, sem).wait()

        @pl.when(mixed == 0)
        def _():
            most = outgoing.at[:, pl.ds(0, EXPERTS - 1)]
            pltpu.make_async_copy(most, most, sem).wait()


def per_device(tokens, route, gate_score, w_gate, w_up, w_down):
    count, width = tokens.shape
    features, units = w_gate.shape[1:]
    bf16, f32 = jnp.bfloat16, jnp.float32
    dma = pltpu.SemaphoreType.DMA
    result = pl.pallas_call(
        kernel,
        out_shape=jax.ShapeDtypeStruct((width, count), bf16),
        in_specs=[pl.BlockSpec(memory_space=pltpu.VMEM)] * 3 + [pl.BlockSpec(memory_space=pl.ANY)] * 3,
        out_specs=pl.BlockSpec(memory_space=pltpu.VMEM),
        scratch_shapes=[
            pltpu.VMEM((SLOTS, count), bf16),
            pltpu.VMEM((2, EXPERTS, CAP // 4, 4, 128), bf16),
            pltpu.VMEM((2, 2, EXPERTS // 2, CAP // 4, 4, 128), bf16),
            pltpu.VMEM((NY, 2, HALF, 128), bf16),
            pltpu.VMEM((NY, 2, HALF // PACK, PACK * (width - 128)), bf16),
            pltpu.VMEM((features, units), bf16),
            pltpu.VMEM((features, units), bf16),
            pltpu.VMEM((features, units), bf16),
            pltpu.VMEM((features, units), bf16),
            pltpu.VMEM((NY, 2 * units, WIDE), bf16),
            pltpu.VMEM((2, HALF, 2 * units), f32),
            pltpu.VMEM((NY, 2, HALF, units), bf16),
            pltpu.VMEM((HALF, WIDE), f32),
            pltpu.VMEM((2, 2, EXPERTS // 2, CAP // 4, 4, 128), bf16),
            pltpu.VMEM((2, EXPERTS, CAP // 4, 4, 128), bf16),
            dma, dma, dma, dma,
            dma((2,)), dma((2, PIECES)), dma((2, PIECES)),
            dma((NY,)), dma((NY,)),
            dma((NY,)), dma((NY,)),
            dma((2, NY // 2, 4)), dma((2, NY // 2, 4)),
            dma((2, NY // 2, 4)), dma((2, NY // 2, 4)),
            pltpu.SemaphoreType.REGULAR((NZ // 2,)),
        ],
        compiler_params=pltpu.CompilerParams(collective_id=0, has_side_effects=True),
        name="experts",
    )(tokens.T, route.T, gate_score.T, w_gate[0], w_up[0], w_down[0])
    return result.T


def solution(mesh):
    split = Mesh(mesh.devices.reshape(2, NZ, 2, NY, 2), EXPERT + BLK)
    return jax.shard_map(
        per_device,
        mesh=split,
        in_specs=(
            P(EXPERT, BLK),
            P(EXPERT, None),
            P(EXPERT, None),
            P(EXPERT, None, BLK),
            P(EXPERT, None, BLK),
            P(EXPERT, BLK, None),
        ),
        out_specs=P(EXPERT, BLK),
        check_vma=False,
    )
```
